32 devices in a mesh: grp: 8 (over z, x), seq: 4 (over y, core).
Axes of the slice: x: 2, y: 2, z: 4, core: 2. Of those that a mesh axis runs over, the one named last changes fastest.
Arguments:
- frames_in: bfloat16 [8192, 512], P(('grp', 'seq')), may hold values from -6 to 6
- norm_gain: float32 [512], replicated, may hold values from 0.25 to 1.75
- qkv_weight: bfloat16 [512, 1536], replicated, may hold values from -0.25 to 0.25
- conv_weight: float32 [4, 1536], replicated, may hold values from -3 to 3
- out_weight: bfloat16 [512, 512], replicated, may hold values from -0.25 to 0.25
- head_gain: float32 [512], replicated, may hold values from 0.25 to 1.75
- ffn_gain: float32 [512], replicated, may hold values from 0.25 to 1.75
- up_weight: bfloat16 [512, 2048], P(None, 'seq'), may hold values from -0.25 to 0.25
- down_weight: bfloat16 [2048, 512], P('seq'), may hold values from -0.125 to 0.125
Outputs:
- encoded: bfloat16 [8192, 512], P(('grp', 'seq'))
The draws below stay inside these ranges and needn't reach their ends.
All inputs are finite; a program needn't handle non-finite values.
Results may differ from the reference program's by a relative error of at most 0.007.
Values may be sent and summed in bfloat16 or wider, within the bound.
No kernel may reach another device: no remote copies, remote signals or barrier semaphores. Data moves between devices by JAX's collectives and lax.ppermute only.
A program may use at most 256 MiB of HBM per device.

```python
import jax
import jax.numpy as jnp
from jax import lax

D = 512
HEADS = 8
HEAD = 64
FF = 2048
KERNEL = 4
BLOCK = 256
FRAMES = 8192


def steps_of(stream_key, shape, shards, least, high):
    level = 1.0
    for position, shards_of in shards:
        draws = jax.random.uniform(jax.random.fold_in(jax.random.fold_in(stream_key, 6), position), (shards_of,), jnp.float32, least / len(shards), high / len(shards))
        level = level * jnp.repeat(jnp.exp(draws), shape[position] // shards_of).reshape((-1,) + (1,) * (len(shape) - 1 - position))
    return level


def centred(key, extent, scale, limit, pieces=(), held_as=jnp.bfloat16):
    entries = scale * jax.random.normal(key, extent, jnp.float32)
    if pieces:
        entries = entries * steps_of(key, extent, pieces, -0.22, 0.18)
    return jnp.clip(entries, -limit, limit).astype(held_as)


def setup_inputs(seed: int = 0) -> dict:
    keys = jax.random.split(jax.random.key(seed), 10)
    return {
        "frames_in": centred(keys[0], (FRAMES, D), 1.0, 6.0, ((0, 32),)),
        "norm_gain": jnp.clip(1.0 + 0.15 * jax.random.normal(keys[1], (D,), jnp.float32), 0.25, 1.75),
        "qkv_weight": centred(keys[2], (D, 3 * D), D ** -0.5, 0.25),
        "conv_weight": centred(keys[3], (KERNEL, 3 * D), KERNEL ** -0.5, 3.0, (), jnp.float32),
        "out_weight": centred(keys[4], (D, D), D ** -0.5, 0.25),
        "head_gain": jnp.clip(1.0 + 0.15 * jax.random.normal(keys[5], (D,), jnp.float32), 0.25, 1.75),
        "ffn_gain": jnp.clip(1.0 + 0.15 * jax.random.normal(keys[6], (D,), jnp.float32), 0.25, 1.75),
        "up_weight": centred(keys[7], (D, FF), D ** -0.5, 0.25, ((1, 4),)),
        "down_weight": centred(keys[8], (FF, D), FF ** -0.5, 0.125, ((0, 4),)),
    }


EPSILON = 1e-05

def rms_scale(values_in, gain):
    mean_square = lax.optimization_barrier(jnp.mean(values_in * values_in, axis=-1, keepdims=True))
    return values_in * lax.rsqrt(mean_square + EPSILON) * gain

def reference(frames_in, norm_gain, qkv_weight, conv_weight, out_weight, head_gain, ffn_gain, up_weight, down_weight):
    model_width = frames_in.shape[1]
    lag_rows = KERNEL - 1
    blocks_in = frames_in.reshape(FRAMES // BLOCK, BLOCK, model_width)
    causal = jnp.arange(BLOCK)[:, None] >= jnp.arange(BLOCK)[None, :]
    highest = lax.Precision.HIGHEST

    def block_step(carried, block_in):
        state_sum, tail_rows = carried
        normed = rms_scale(block_in.astype(jnp.float32), norm_gain).astype(jnp.bfloat16)
        projected = jnp.dot(normed, qkv_weight, preferred_element_type=jnp.float32).astype(jnp.bfloat16)
        extended = jnp.concatenate([tail_rows, projected], axis=0).astype(jnp.float32)
        convolved = jnp.zeros((BLOCK, 3 * model_width), jnp.float32)
        for offset in range(KERNEL):
            convolved = convolved + conv_weight[offset] * extended[lag_rows - offset:lag_rows - offset + BLOCK]
        queries = jax.nn.silu(convolved[:, :model_width]).astype(jnp.bfloat16)
        key_rows = jax.nn.silu(convolved[:, model_width:2 * model_width]).astype(jnp.bfloat16)
        value_rows = convolved[:, 2 * model_width:].astype(jnp.bfloat16)
        query_wide = queries.astype(jnp.float32).reshape(BLOCK, HEADS, HEAD)
        key_wide = key_rows.astype(jnp.float32).reshape(BLOCK, HEADS, HEAD)
        value_wide = value_rows.astype(jnp.float32).reshape(BLOCK, HEADS, HEAD)
        state_low = state_sum.astype(jnp.bfloat16).astype(jnp.float32)
        scores = jnp.einsum('thd,shd->hts', query_wide, key_wide, precision=highest)
        scores = jnp.where(causal[None], scores, 0.0).astype(jnp.bfloat16).astype(jnp.float32)
        local_part = jnp.einsum('hts,shd->thd', scores, value_wide, precision=highest)
        carried_part = jnp.einsum('thd,hde->the', query_wide, state_low, precision=highest)
        attended = local_part + carried_part
        head_square = lax.optimization_barrier(jnp.mean(attended * attended, axis=-1, keepdims=True))
        headed = (attended * lax.rsqrt(head_square + EPSILON)).reshape(BLOCK, model_width) * head_gain
        headed = headed.astype(jnp.bfloat16)
        residual = block_in.astype(jnp.float32) + jnp.dot(headed, out_weight, preferred_element_type=jnp.float32)
        normed_ffn = rms_scale(residual, ffn_gain).astype(jnp.bfloat16)
        inner_act = jax.nn.gelu(jnp.dot(normed_ffn, up_weight, preferred_element_type=jnp.float32)).astype(jnp.bfloat16)
        encoded = (residual + jnp.dot(inner_act, down_weight, preferred_element_type=jnp.float32)).astype(jnp.bfloat16)
        next_state = state_sum + jnp.einsum('shd,she->hde', key_wide, value_wide, precision=highest)
        return ((next_state, projected[BLOCK - lag_rows:]), encoded)
    initial = (jnp.zeros((HEADS, HEAD, HEAD), jnp.float32), jnp.zeros((lag_rows, 3 * model_width), jnp.bfloat16))
    unused, outputs = lax.scan(block_step, initial, blocks_in)
    return outputs.reshape(FRAMES, model_width)
```

```python
import functools

import jax
import jax.numpy as jnp
from jax import lax
from jax.experimental import pallas as pl
from jax.experimental.pallas import tpu as pltpu
from jax.sharding import PartitionSpec as P

HEADS = 8
HEAD = 64
KERNEL = 4
BLOCK = 256
EPSILON = 1e-05
AXES = ("grp", "seq")
LAG = 8
F32 = jnp.float32
BF16 = jnp.bfloat16


def vmem():
    return pl.BlockSpec(memory_space=pltpu.VMEM)


def dot(a, b):
    return jnp.dot(a, b, preferred_element_type=F32)


def rms_rows(values, gain):
    mean_square = jnp.mean(values * values, axis=-1, keepdims=True)
    return values * lax.rsqrt(mean_square + EPSILON) * gain


def project_kernel(frames_ref, gain_ref, weight_ref, out_ref, tail_ref):
    rows = frames_ref.shape[0]
    normed = rms_rows(frames_ref[...].astype(F32), gain_ref[...]).astype(BF16)
    projected = dot(normed, weight_ref[...]).astype(BF16)
    out_ref[...] = projected
    tail_ref[...] = projected[rows - 2 * LAG :].astype(F32)[LAG:].astype(BF16)


def lanes(shape, dim):
    return lax.broadcasted_iota(jnp.int32, shape, dim)


def convolve_kernel(
    projected_ref, before_ref, taps_ref, q_ref, k_ref, v_ref, state_ref, extended
):
    rows, channels = projected_ref.shape
    width = channels // 3
    extended[:LAG, :] = before_ref[...].astype(F32)
    extended[LAG:, :] = projected_ref[...].astype(F32)
    for part, ref in enumerate((q_ref, k_ref, v_ref)):
        at = slice(part * width, (part + 1) * width)
        total = jnp.zeros((rows, width), F32)
        for offset in range(KERNEL):
            total = total + taps_ref[offset : offset + 1, at] * extended[LAG - offset : LAG - offset + rows, at]
        if part < 2:
            total = total / (1.0 + jnp.exp(-total))
        ref[...] = total.astype(BF16)
    half = width // 2
    folded = []
    same = lanes((half, half), 0) // HEAD == lanes((half, half), 1) // HEAD
    for g in range(2):
        at = slice(g * half, (g + 1) * half)
        outer = lax.dot_general(
            k_ref[:, at], v_ref[:, at], (((0,), (0,)), ((), ())), preferred_element_type=F32
        )
        outer = jnp.where(same, outer, 0.0)
        fold = outer[:, : 2 * HEAD]
        for start in range(2 * HEAD, half, 2 * HEAD):
            fold = fold + outer[:, start : start + 2 * HEAD]
        folded.append(fold + pltpu.roll(fold, HEAD, 1))
    low = lanes(folded[0].shape, 1) < HEAD
    state_ref[...] = jnp.where(low, folded[0], folded[1])


def local_kernel(q_ref, k_ref, v_ref, out_ref):
    rows = q_ref.shape[0]
    causal = lanes((rows, rows), 0) >= lanes((rows, rows), 1)
    pair = 2 * HEAD
    first = lanes((rows, pair), 1) < HEAD
    for p in range(HEADS // 2):
        at = slice(p * pair, (p + 1) * pair)
        q, k, v = q_ref[:, at], k_ref[:, at], v_ref[:, at]
        total = None
        for side in range(2):
            mine = first if side == 0 else jnp.logical_not(first)
            zero = jnp.zeros_like(k)
            scores = lax.dot_general(
                q, jnp.where(mine, k, zero), (((1,), (1,)), ((), ())), preferred_element_type=F32
            )
            scores = jnp.where(causal, scores, 0.0).astype(BF16)
            part = dot(scores, jnp.where(mine, v, zero))
            total = part if total is None else total + part
        out_ref[:, at] = total


def gelu(x):
    return 0.5 * x * (1.0 + jnp.tanh(0.7978845608028654 * (x + 0.044715 * (x * x * x))))


def tail_kernel(count, *refs):
    (q_ref, local_ref, state_ref, frames_ref, head_gain_ref, ffn_gain_ref, out_w_ref) = refs[:7]
    ups, downs = refs[7 : 7 + count], refs[7 + count : 7 + 2 * count]
    out_ref = refs[7 + 2 * count]
    up_buf, down_buf, up_sem, down_sem = refs[8 + 2 * count :]
    copies = []
    for i in range(count):
        a = pltpu.make_async_copy(ups[i], up_buf.at[i], up_sem.at[i])
        b = pltpu.make_async_copy(downs[i], down_buf.at[i], down_sem.at[i])
        a.start()
        b.start()
        copies.append((a, b))
    width = q_ref.shape[1]
    half = width // 2
    state = state_ref[...]
    turned = pltpu.roll(state, HEAD, 1)
    low = lanes(state.shape, 1) < HEAD
    same = lanes((half, half), 0) // HEAD == lanes((half, half), 1) // HEAD
    mean_of = jnp.where(same, 1.0 / HEAD, 0.0).astype(BF16)
    headed = []
    for g in range(2):
        at = slice(g * half, (g + 1) * half)
        both = jnp.where(low, state, turned) if g == 0 else jnp.where(low, turned, state)
        spread = jnp.concatenate([both] * (half // (2 * HEAD)), axis=1)
        spread = jnp.where(same, spread, 0.0).astype(BF16)
        attended = local_ref[:, at] + dot(q_ref[:, at], spread)
        square = attended * attended
        upper = square.astype(BF16)
        lower = (square - upper.astype(F32)).astype(BF16)
        mean = dot(upper, mean_of) + dot(lower, mean_of)
        headed.append(
            (attended * lax.rsqrt(mean + EPSILON) * head_gain_ref[:, at]).astype(BF16)
        )
    residual = frames_ref[...].astype(F32) + dot(jnp.concatenate(headed, axis=1), out_w_ref[...])
    normed = rms_rows(residual, ffn_gain_ref[...]).astype(BF16)
    total = residual
    for i in range(count):
        copies[i][0].wait()
        inner = gelu(dot(normed, up_buf[i])).astype(BF16)
        copies[i][1].wait()
        total = total + dot(inner, down_buf[i])
    out_ref[...] = total.astype(BF16)


def shapes(*pairs):
    return tuple(jax.ShapeDtypeStruct(s, d) for s, d in pairs)


def swap(value, bit, count):
    return lax.ppermute(value, AXES, [(i, i ^ bit) for i in range(count)])


def body(
    devices,
    seqs,
    frames_in,
    norm_gain,
    qkv_weight,
    conv_weight,
    out_weight,
    head_gain,
    ffn_gain,
    up_weight,
    down_weight,
):
    rows, width = frames_in.shape
    place = lax.axis_index(AXES)
    projected, tail = pl.pallas_call(
        project_kernel,
        out_shape=shapes(((rows, 3 * width), BF16), ((LAG, 3 * width), BF16)),
        in_specs=[vmem()] * 3,
        out_specs=(vmem(), vmem()),
        name="project",
    )(frames_in, norm_gain.reshape(1, -1), qkv_weight)
    before = lax.ppermute(tail, AXES, [(i, i + 1) for i in range(devices - 1)])
    queries, key_rows, value_rows, state = pl.pallas_call(
        convolve_kernel,
        out_shape=shapes(*[((rows, width), BF16)] * 3, ((width // 2, 2 * HEAD), F32)),
        in_specs=[vmem()] * 3,
        out_specs=(vmem(),) * 4,
        scratch_shapes=[pltpu.VMEM((LAG + rows, 3 * width), F32)],
        name="convolve",
    )(projected, before, conv_weight)

    own = (up_weight, down_weight)
    total, prefix = state, jnp.zeros_like(state)
    bit = 1
    while bit < devices:
        came = swap(total.astype(BF16), bit, devices).astype(F32)
        prefix = prefix + jnp.where((place & bit) != 0, came, 0.0)
        total = total + came
        if bit == seqs // 2:
            own, total = lax.optimization_barrier((own, total))
        bit *= 2

    local = pl.pallas_call(
        local_kernel,
        out_shape=jax.ShapeDtypeStruct((rows, width), F32),
        in_specs=[vmem()] * 3,
        out_specs=vmem(),
        name="local",
    )(queries, key_rows, value_rows)

    sets = [own]
    bit = 2
    while bit < seqs:
        sets = sets + [tuple(swap(w, bit, devices) for w in s) for s in sets]
        bit *= 2
    if seqs > 1:
        sets = [
            t
            for s in sets
            for t in (s, tuple(swap(w, 1, devices) for w in s))
        ]
    count = len(sets)
    hidden = up_weight.shape[1]
    anywhere = pl.BlockSpec(memory_space=pl.ANY)
    return pl.pallas_call(
        functools.partial(tail_kernel, count),
        out_shape=jax.ShapeDtypeStruct((rows, width), BF16),
        in_specs=[vmem()] * 7 + [anywhere] * (2 * count),
        out_specs=vmem(),
        scratch_shapes=[
            pltpu.VMEM((count, width, hidden), BF16),
            pltpu.VMEM((count, hidden, width), BF16),
            pltpu.SemaphoreType.DMA((count,)),
            pltpu.SemaphoreType.DMA((count,)),
        ],
        name="tail",
    )(
        queries,
        local,
        prefix,
        frames_in,
        head_gain.reshape(1, -1),
        ffn_gain.reshape(1, -1),
        out_weight,
        *[s[0] for s in sets],
        *[s[1] for s in sets],
    )


def solution(mesh):
    sizes = dict(mesh.shape)
    in_specs = (
        P(AXES, None),
        P(),
        P(),
        P(),
        P(),
        P(),
        P(),
        P(None, "seq"),
        P("seq", None),
    )
    return jax.shard_map(
        functools.partial(body, sizes["grp"] * sizes["seq"], sizes["seq"]),
        mesh=mesh,
        in_specs=in_specs,
        out_specs=P(AXES, None),
        check_vma=False,
    )
```
